32 devices in a mesh: chan: 4 (over z), slab: 2 (over core), batch: 4 (over y, x).
Axes of the slice: x: 2, y: 2, z: 4, core: 2. Of those that a mesh axis runs over, the one named last changes fastest.
Arguments:
- inputs: bfloat16 [2048, 8, 512], P(('batch', 'chan'), 'slab'), parts along dimension 0, may hold values from -6 to 6
- weights: bfloat16 [27, 512, 512], P(None, 'chan'), may hold values from -0.0625 to 0.0625
- out_grad: bfloat16 [2048, 8, 512], P(('batch', 'chan'), 'slab'), parts along dimension 0, may hold values from -6 to 6
Outputs:
- conv_out: bfloat16 [2048, 8, 512], P(('batch', 'chan'), 'slab'), parts along dimension 0
- input_grad: bfloat16 [2048, 8, 512], P(('batch', 'chan'), 'slab'), parts along dimension 0
The draws below stay inside these ranges and needn't reach their ends.
There are 4 independent parts, one for each index of `batch`. The reference program is written for one: setup_inputs(seed, part) draws one part's arguments, and reference() takes and returns one part's arrays. A program takes and returns all parts, laid end to end along the dimension named above; an argument that names none is the same for every part. Nothing has to cross between parts.
All inputs are finite; a program needn't handle non-finite values.
Results may differ from the reference program's by a relative error of at most 0.0013.
Values may be sent and summed in bfloat16 or wider, within the bound.
No kernel may reach another device: no remote copies, remote signals or barrier semaphores. Data moves between devices by JAX's collectives and lax.ppermute only.
A program may use at most 192 MiB of HBM per device.

```python
import jax
import jax.numpy as jnp
from jax import lax

CIN = 512
COUT = 512
NY = 8
NZ = 64
NX = 8


def with_spikes(result, key, source, target, shards_of, factor):
    owner, partner = [(jnp.arange(result.shape[dim]) // (result.shape[dim] // shards_of)).reshape([-1 if axis == dim else 1 for axis in range(result.ndim)]) for dim in (source, target)]
    chosen = jax.random.permutation(key, shards_of)[partner]
    strong = (owner == chosen) | (owner == (partner + shards_of // 2) % shards_of)
    return jnp.where(strong, factor * result, result)


def shard_levels(stream_key, extent, cuts, smallest, top_value):
    gain, own = 1.0, jax.random.fold_in(stream_key, 6)
    for axis_at, blocks in cuts:
        heights = jnp.exp(jax.random.uniform(jax.random.fold_in(own, axis_at), (blocks,), jnp.float32, smallest / len(cuts), top_value / len(cuts)))
        gain = gain * jnp.repeat(heights, extent[axis_at] // blocks).reshape([-1 if axis == axis_at else 1 for axis in range(len(extent))])
    return gain


def scatter_about(stream_key, shape, spread, most, shards=(), kind=jnp.bfloat16):
    result = jax.random.normal(stream_key, shape, jnp.float32) * spread
    if len(shards) > 0:
        result = shard_levels(stream_key, shape, shards, -0.22, 0.18) * result
    return jnp.clip(result, min=-most, max=most).astype(kind)


def bell_draw_with(rng, shape, scale, bound, shards, heavy, dtype=jnp.bfloat16):
    values = scale * jax.random.normal(rng, shape, jnp.float32)
    if shards:
        values = values * shard_levels(rng, shape, shards, -0.22, 0.18)
    return jnp.clip(with_spikes(values, jax.random.fold_in(rng, 3), *heavy), -bound, bound).astype(dtype)


def setup_inputs(seed: int = 0, part: int = 0) -> dict:
    splits = jax.random.split(jax.random.key(seed), 4)
    part_keys = jax.random.split(jax.random.fold_in(splits[3], part), 4)
    inputs = scatter_about(part_keys[0], (CIN, NX, NY * NZ), 1.0, 6.0, ((0, 4), (1, 2)))
    weights = bell_draw_with(splits[1], (27, CIN, COUT), (27 * CIN) ** -0.5, 0.0625, ((1, 4),), (1, 2, 4, 2.0))
    out_grad = scatter_about(part_keys[2], (COUT, NX, NY * NZ), 1.0, 6.0, ((0, 4), (1, 2)))
    return dict(inputs=inputs, weights=weights, out_grad=out_grad)


OFFSETS = (-1, 0, 1)


def reference(inputs, weights, out_grad):
    field_in = inputs.astype(jnp.float32).reshape(CIN, NX, NY, NZ)
    field_grad = out_grad.astype(jnp.float32).reshape(COUT, NX, NY, NZ)
    kernel = weights.astype(jnp.float32)
    forward = jnp.zeros((COUT, NX, NY, NZ), jnp.float32)
    backward = jnp.zeros((CIN, NX, NY, NZ), jnp.float32)
    for offset_x in OFFSETS:
        for offset_y in OFFSETS:
            for offset_z in OFFSETS:
                number = 9 * (offset_x + 1) + 3 * (offset_y + 1) + (offset_z + 1)
                moved_in = jnp.roll(field_in, (-offset_x, -offset_y, -offset_z), axis=(1, 2, 3))
                forward = forward + jnp.einsum("io,ixyz->oxyz", kernel[number], moved_in, precision=lax.Precision.HIGHEST)
                moved_grad = jnp.roll(field_grad, (offset_x, offset_y, offset_z), axis=(1, 2, 3))
                backward = backward + jnp.einsum("io,oxyz->ixyz", kernel[number], moved_grad, precision=lax.Precision.HIGHEST)
    conv_out = forward.reshape(COUT, NX, NY * NZ).astype(jnp.bfloat16)
    input_grad = backward.reshape(CIN, NX, NY * NZ).astype(jnp.bfloat16)
    return (conv_out, input_grad)
```

```python
import functools

import jax
import jax.numpy as jnp
from jax import lax
from jax.experimental import pallas as pl
from jax.experimental.pallas import tpu as pltpu
from jax.sharding import PartitionSpec as P

NZ = 64
OFFSETS = (-1, 0, 1)
VMEM_LIMIT = 56 * 2**20

def shift_z(block, offset):
    if offset == 0:
        return block
    lanes = block.shape[1]
    z = lax.broadcasted_iota(jnp.int32, block.shape, 1) % NZ
    plain = pltpu.roll(block, offset % lanes, 1)
    wrapped = pltpu.roll(block, (offset - NZ * offset) % lanes, 1)
    edge = z == (0 if offset == 1 else NZ - 1)
    return jnp.where(edge, wrapped, plain)

def shift_y(block, offset):
    if offset == 0:
        return block
    return pltpu.roll(block, (NZ * offset) % block.shape[1], 1)

def forward_kernel(slab, halo_ref, x_ref, w_ref, out_ref, columns, wt):
    plane = pl.program_id(0)
    chans, size = w_ref.shape[1], out_ref.shape[1]

    @pl.when(plane == 0)
    def _():
        for o in range(27):
            wt[:, o * chans:(o + 1) * chans] = w_ref[o].T
        for p in range(slab + 2):
            if p == 0:
                source = halo_ref[:, :size]
            elif p == slab + 1:
                source = halo_ref[:, size:]
            else:
                source = x_ref[:, (p - 1) * size:p * size]
            for iz, offset_z in enumerate(OFFSETS):
                moved = shift_z(source, -offset_z)
                for iy, offset_y in enumerate(OFFSETS):
                    row = (3 * iy + iz) * chans
                    columns[row:row + chans, p * size:(p + 1) * size] = shift_y(moved, -offset_y)

    total = None
    for ix in range(3):
        at = pl.multiple_of((plane + ix) * size, size)
        part = jnp.dot(wt[:, ix * 9 * chans:(ix + 1) * 9 * chans], columns[:, pl.ds(at, size)],
                       preferred_element_type=jnp.float32)
        total = part if total is None else total + part
    out_ref[...] = total

def forward(x, halo, w, slab):
    chans, cells = x.shape
    size = cells // slab
    full = w.shape[2]
    whole = lambda a: pl.BlockSpec(a.shape, lambda n: (0,) * a.ndim, pipeline_mode=pl.Buffered(1))
    return pl.pallas_call(
        functools.partial(forward_kernel, slab),
        grid=(slab,),
        in_specs=[whole(halo), whole(x), whole(w)],
        out_specs=pl.BlockSpec((full, size), lambda n: (0, n)),
        out_shape=jax.ShapeDtypeStruct((full, cells), jnp.float32),
        scratch_shapes=[pltpu.VMEM((9 * chans, (slab + 2) * size), jnp.bfloat16),
                        pltpu.VMEM((full, 27 * chans), jnp.bfloat16)],
        compiler_params=pltpu.CompilerParams(vmem_limit_bytes=VMEM_LIMIT),
        cost_estimate=pl.CostEstimate(flops=2*27*chans*full*cells, bytes_accessed=w.size*2+full*cells*4, transcendentals=0),
        name="forward",
    )(halo, x, w)

def backward_kernel(slab, number, first, where_ref, *refs):
    halos, blocks = refs[:number], refs[number:2 * number]
    w_ref = refs[2 * number]
    before = None if first else refs[2 * number + 1]
    out_ref, lhs, rhs = refs[-3:]
    plane = pl.program_id(0)
    chans_in, size = w_ref.shape[1], out_ref.shape[1]
    chans = blocks[0].shape[0]

    @pl.when(plane == 0)
    def _():
        for k in range(number):
            at = pl.multiple_of(where_ref[k] * chans, chans)
            for ix, offset_x in enumerate(OFFSETS):
                row = (3 * k + ix) * chans
                for o in range(9):
                    lhs[o * chans_in:(o + 1) * chans_in, row:row + chans] = w_ref[9 * ix + o, :, pl.ds(at, chans)]
                if offset_x == 0:
                    rhs[row:row + chans, :] = blocks[k][...]
                elif offset_x == 1:
                    rhs[row:row + chans, :size] = halos[k][:, :size]
                    rhs[row:row + chans, size:] = blocks[k][:, :(slab - 1) * size]
                else:
                    rhs[row:row + chans, :(slab - 1) * size] = blocks[k][:, size:]
                    rhs[row:row + chans, (slab - 1) * size:] = halos[k][:, size:]

    at = pl.multiple_of(plane * size, size)
    total = None if first else before[...]
    for iz, offset_z in enumerate(OFFSETS):
        over_y = None
        for iy, offset_y in enumerate(OFFSETS):
            row = (3 * iy + iz) * chans_in
            part = jnp.dot(lhs[row:row + chans_in, :], rhs[:, pl.ds(at, size)], preferred_element_type=jnp.float32)
            part = shift_y(part, offset_y)
            over_y = part if over_y is None else over_y + part
        over_y = shift_z(over_y, offset_z)
        total = over_y if total is None else total + over_y
    out_ref[...] = total.astype(out_ref.dtype)

def backward(where, blocks, halos, w, before, slab, out_dtype):
    number = len(blocks)
    chans, cells = blocks[0].shape
    chans_in = w.shape[1]
    size = cells // slab
    first = before is None
    whole = lambda a: pl.BlockSpec(a.shape, lambda n, s: (0,) * a.ndim, pipeline_mode=pl.Buffered(1))
    each = pl.BlockSpec((chans_in, size), lambda n, s: (0, n))
    args = (*halos, *blocks, w) + (() if first else (before,))
    return pl.pallas_call(
        functools.partial(backward_kernel, slab, number, first),
        grid_spec=pltpu.PrefetchScalarGridSpec(
            num_scalar_prefetch=1, grid=(slab,),
            in_specs=[whole(a) for a in args[:2 * number + 1]] + ([] if first else [each]),
            out_specs=each,
            scratch_shapes=[pltpu.VMEM((9 * chans_in, 3 * number * chans), jnp.bfloat16),
                            pltpu.VMEM((3 * number * chans, cells), jnp.bfloat16)]),
        out_shape=jax.ShapeDtypeStruct((chans_in, cells), out_dtype),
        compiler_params=pltpu.CompilerParams(vmem_limit_bytes=VMEM_LIMIT),
        cost_estimate=pl.CostEstimate(flops=2*27*chans*chans_in*cells*number, bytes_accessed=w.size*2+chans_in*cells*4, transcendentals=0),
        name="backward",
    )(where, *args)


def padded(block, sides, width):
    for axis, dim in sides:
        count = lax.axis_size(axis)
        forward_ring = [(i, (i + 1) % count) for i in range(count)]
        backward_ring = [(target, source) for source, target in forward_ring]
        low = lax.ppermute(
            lax.slice_in_dim(block, block.shape[dim] - width, None, axis=dim), axis, forward_ring
        )
        high = lax.ppermute(lax.slice_in_dim(block, 0, width, axis=dim), axis, backward_ring)
        block = jnp.concatenate([low, block, high], axis=dim)
    return block


def stack_yz(block, rows_y):
    chans, slab_len, plane_size = block.shape
    shaped = block.reshape(chans, slab_len, rows_y, NZ)
    pieces = []
    for offset_y in OFFSETS:
        for offset_z in OFFSETS:
            pieces.append(jnp.roll(shaped, (-offset_y, -offset_z), axis=(2, 3)))
    return jnp.stack(pieces).reshape(9 * chans, slab_len * plane_size)


def general(inputs, weights, out_grad):
    chans_in, slab_len, plane_size = inputs.shape
    chans_out = out_grad.shape[0]
    full_out = weights.shape[2]
    rows_y = plane_size // NZ
    cell_count = slab_len * plane_size
    halo_in = padded(inputs, (("slab", 1),), 1)
    grad_all = lax.all_gather(out_grad, "chan", axis=0, tiled=True)
    halo_grad = padded(grad_all, (("slab", 1),), 1)
    running = jnp.zeros((full_out, cell_count), jnp.float32)
    for index_x, offset_x in enumerate(OFFSETS):
        columns = stack_yz(halo_in[:, 1 + offset_x : 1 + offset_x + slab_len], rows_y)
        weight_x = weights[9 * index_x : 9 * index_x + 9].reshape(9 * chans_in, full_out)
        running = running + lax.dot_general(
            weight_x, columns, (((0,), (0,)), ((), ())), preferred_element_type=jnp.float32
        )
    own_rows = lax.psum_scatter(running, "chan", scatter_dimension=0, tiled=True)
    conv_out = own_rows.astype(jnp.bfloat16).reshape(chans_out, slab_len, plane_size)
    running_grad = jnp.zeros((chans_in, slab_len, rows_y, NZ), jnp.float32)
    for index_x, offset_x in enumerate(OFFSETS):
        plane_x = halo_grad[:, 1 - offset_x : 1 - offset_x + slab_len].reshape(full_out, cell_count)
        weight_x = weights[9 * index_x : 9 * index_x + 9].reshape(9 * chans_in, full_out)
        product = lax.dot_general(
            weight_x, plane_x, (((1,), (0,)), ((), ())), preferred_element_type=jnp.float32
        )
        product = product.reshape(9, chans_in, slab_len, rows_y, NZ)
        for index_y, offset_y in enumerate(OFFSETS):
            for index_z, offset_z in enumerate(OFFSETS):
                running_grad = running_grad + jnp.roll(
                    product[3 * index_y + index_z], (offset_y, offset_z), axis=(2, 3)
                )
    input_grad = running_grad.reshape(chans_in, slab_len, plane_size).astype(jnp.bfloat16)
    return (conv_out, input_grad)


def edge_planes(block, size):
    count = lax.axis_size("slab")
    first, last = block[:, :size], block[:, block.shape[1] - size :]
    upward = [(i, (i + 1) % count) for i in range(count)]
    if count <= 2:
        return lax.ppermute(jnp.concatenate([last, first], axis=1), "slab", upward)
    downward = [(target, source) for source, target in upward]
    low, high = lax.ppermute(last, "slab", upward), lax.ppermute(first, "slab", downward)
    return jnp.concatenate([low, high], axis=1)


MARK_ROWS = 8


def pack(total):
    top = jnp.max(jnp.abs(total))
    power = jnp.clip(jnp.ceil(jnp.log2(jnp.maximum(top, 1e-36))), -100.0, 100.0)
    scaled = (total * jnp.exp2(15.0 - power)).astype(jnp.float16)
    mark = jnp.full((MARK_ROWS, total.shape[1]), power, jnp.float16)
    return jnp.concatenate([scaled, mark], axis=0)


def unpack(parcel):
    rows = parcel.shape[0] - MARK_ROWS
    power = parcel[rows, 0].astype(jnp.float32)
    return parcel[:rows].astype(jnp.float32) * jnp.exp2(power - 15.0)


def line_of_four(inputs, weights, out_grad):
    chans, slab_len, size = inputs.shape
    cells = slab_len * size
    place = lax.axis_index("chan")
    move = lambda a, pairs: lax.ppermute(a, "chan", pairs)
    pick = lambda *options: jnp.asarray(options, jnp.int32)[place]
    middle = (place == 1) | (place == 2)

    grad = out_grad.reshape(chans, cells)
    field = inputs.reshape(chans, cells)
    from_below = move(grad, [(0, 1), (1, 2), (2, 3)])
    from_above = move(grad, [(1, 0), (2, 1), (3, 2)])
    field_edges = edge_planes(field, size)
    grad_edges = edge_planes(grad, size)

    partial = forward(field, field_edges, weights, slab_len)
    block = lambda index: lax.dynamic_slice_in_dim(partial, index * chans, chans, axis=0)

    sum_1 = move(pack(block(pick(3, 3, 0, 0))), [(0, 1), (3, 2)])
    below_2 = move(from_below, [(1, 2), (2, 3)])
    above_2 = move(from_above, [(2, 1), (1, 0)])
    second = jnp.where(place == 0, from_above, from_below)
    second_edges = edge_planes(second, size)
    grad_half = backward(
        jnp.stack([place, pick(1, 0, 1, 2)]), (grad, second), (grad_edges, second_edges),
        weights, None, slab_len, jnp.float32,
    )

    parcel = pack(block(pick(2, 3, 0, 1)) + unpack(sum_1))
    sum_below = move(parcel, [(0, 1), (1, 2)])
    sum_above = move(parcel, [(3, 2), (2, 1)])
    relayed = jnp.where(place >= 2, below_2, above_2)
    far = move(relayed, [(2, 3), (1, 0)])
    third = jnp.where(middle, from_above, relayed)
    fourth = jnp.where(middle, relayed, far)
    third_edges = edge_planes(third, size)
    fourth_edges = edge_planes(fourth, size)

    last_below = move(pack(block(pick(1, 2, 3, 3)) + unpack(sum_below)), [(0, 1), (1, 2), (2, 3)])
    last_above = move(pack(block(pick(0, 0, 1, 2)) + unpack(sum_above)), [(3, 2), (2, 1), (1, 0)])
    input_grad = backward(
        jnp.stack([pick(2, 2, 3, 1), pick(3, 3, 0, 0)]), (third, fourth), (third_edges, fourth_edges),
        weights, grad_half, slab_len, jnp.bfloat16,
    )
    conv_out = (block(place) + unpack(last_below) + unpack(last_above)).astype(jnp.bfloat16)
    shape = (chans, slab_len, size)
    return conv_out.reshape(shape), input_grad.reshape(shape)


def per_device(inputs, weights, out_grad):
    chans, size = inputs.shape[0], inputs.shape[2]
    line = lax.axis_size("chan") == 4 and weights.shape[2] == 4 * chans and out_grad.shape[0] == chans
    if line and chans % 128 == 0 and size % 128 == 0:
        return line_of_four(inputs, weights, out_grad)
    return general(inputs, weights, out_grad)


def solution(mesh):
    in_specs = (
        P(("batch", "chan"), "slab", None),
        P(None, "chan", None),
        P(("batch", "chan"), "slab", None),
    )
    out_specs = (P(("batch", "chan"), "slab", None), P(("batch", "chan"), "slab", None))
    return jax.shard_map(
        per_device, mesh=mesh, in_specs=in_specs, out_specs=out_specs, check_vma=False
    )
```

```python
import functools

import jax
import jax.numpy as jnp
from jax import lax
from jax.experimental import pallas as pl
from jax.experimental.pallas import tpu as pltpu
from jax.sharding import PartitionSpec as P


NZ = 64
OFFSETS = (-1, 0, 1)
VMEM_LIMIT = 56 * 2**20


def shift_z(block, offset):
    if offset == 0:
        return block
    lanes = block.shape[1]
    z = lax.broadcasted_iota(jnp.int32, block.shape, 1) % NZ
    plain = pltpu.roll(block, offset % lanes, 1)
    wrapped = pltpu.roll(block, (offset - NZ * offset) % lanes, 1)
    edge = z == (0 if offset == 1 else NZ - 1)
    return jnp.where(edge, wrapped, plain)


def shift_y(block, offset):
    if offset == 0:
        return block
    return pltpu.roll(block, (NZ * offset) % block.shape[1], 1)


def forward_kernel(slab, position_ref, halo_ref, x_ref, w_ref, out_ref, marks_ref, columns, wt, top_ref):
    plane = pl.program_id(0)
    chans, size = w_ref.shape[1], out_ref.shape[1]

    @pl.when(plane == 0)
    def _():
        for o in range(27):
            wt[:, o * chans:(o + 1) * chans] = w_ref[o].T
        for p in range(slab + 2):
            if p == 0:
                source = halo_ref[:, :size]
            elif p == slab + 1:
                source = halo_ref[:, size:]
            else:
                source = x_ref[:, (p - 1) * size:p * size]
            for iz, offset_z in enumerate(OFFSETS):
                moved = shift_z(source, -offset_z)
                for iy, offset_y in enumerate(OFFSETS):
                    row = (3 * iy + iz) * chans
                    columns[row:row + chans, p * size:(p + 1) * size] = shift_y(moved, -offset_y)

    total = None
    for ix in range(3):
        at = pl.multiple_of((plane + ix) * size, size)
        part = jnp.dot(wt[:, ix * 9 * chans:(ix + 1) * 9 * chans], columns[:, pl.ds(at, size)],
                       preferred_element_type=jnp.float32)
        total = part if total is None else total + part
    out_ref[...] = total
    top = jnp.max(jnp.max(jnp.abs(total), axis=0, keepdims=True), axis=1, keepdims=True)
    top = jnp.broadcast_to(top, top_ref.shape)

    @pl.when(plane == 0)
    def _():
        top_ref[...] = top

    @pl.when(plane > 0)
    def _():
        top_ref[...] = jnp.maximum(top_ref[...], top)

    @pl.when(plane == slab - 1)
    def _():
        power = jnp.clip(jnp.ceil(jnp.log2(jnp.maximum(top_ref[...], 1e-30))), -28.0, 15.0)
        high = jnp.maximum(power, -14.0)
        row = lax.broadcasted_iota(jnp.int32, top_ref.shape, 0) - 2 * position_ref[0]
        mark = jnp.where(row == 0, jnp.exp2(high), jnp.where(row == 1, jnp.exp2(power - high), 0.0))
        for lane in range(0, marks_ref.shape[1], mark.shape[1]):
            marks_ref[:, lane : lane + mark.shape[1]] = mark


def forward(position, x, halo, w, slab):
    chans, cells = x.shape
    size = cells // slab
    full = w.shape[2]
    whole = lambda a: pl.BlockSpec(a.shape, lambda n, s: (0,) * a.ndim, pipeline_mode=pl.Buffered(1))
    return pl.pallas_call(
        functools.partial(forward_kernel, slab),
        grid_spec=pltpu.PrefetchScalarGridSpec(
            num_scalar_prefetch=1,
            grid=(slab,),
            in_specs=[whole(halo), whole(x), whole(w)],
            out_specs=[
                pl.BlockSpec((full, size), lambda n, s: (0, n)),
                pl.BlockSpec((8, cells), lambda n, s: (0, 0)),
            ],
            scratch_shapes=[
                pltpu.VMEM((9 * chans, (slab + 2) * size), jnp.bfloat16),
                pltpu.VMEM((full, 27 * chans), jnp.bfloat16),
                pltpu.VMEM((8, 128), jnp.float32),
            ],
        ),
        out_shape=[
            jax.ShapeDtypeStruct((full, cells), jnp.float32),
            jax.ShapeDtypeStruct((8, cells), jnp.float32),
        ],
        compiler_params=pltpu.CompilerParams(vmem_limit_bytes=VMEM_LIMIT),
        cost_estimate=pl.CostEstimate(
            flops=2 * 27 * chans * full * cells,
            bytes_accessed=w.size * 2 + full * cells * 4,
            transcendentals=0,
        ),
        name="forward",
    )(position, halo, x, w)


def backward_kernel(slab, sources, first, position_ref, *refs):
    number = len(sources)
    halos, blocks = refs[:number], refs[number:2 * number]
    w_ref = refs[2 * number]
    before = None if first else refs[2 * number + 1]
    out_ref, lhs, rhs = refs[-3:]
    plane = pl.program_id(0)
    chans_in, size = w_ref.shape[1], out_ref.shape[1]
    chans = blocks[0].shape[0]

    @pl.when(plane == 0)
    def _():
        for k in range(number):
            at = pl.multiple_of(sources[k](position_ref[0]) * chans, chans)
            for ix, offset_x in enumerate(OFFSETS):
                row = (3 * k + ix) * chans
                for o in range(9):
                    lhs[o * chans_in:(o + 1) * chans_in, row:row + chans] = w_ref[9 * ix + o, :, pl.ds(at, chans)]
                if offset_x == 0:
                    rhs[row:row + chans, :] = blocks[k][...]
                elif offset_x == 1:
                    rhs[row:row + chans, :size] = halos[k][:, :size]
                    rhs[row:row + chans, size:] = blocks[k][:, :(slab - 1) * size]
                else:
                    rhs[row:row + chans, :(slab - 1) * size] = blocks[k][:, size:]
                    rhs[row:row + chans, (slab - 1) * size:] = halos[k][:, size:]

    at = pl.multiple_of(plane * size, size)
    total = None if first else before[...]
    for iz, offset_z in enumerate(OFFSETS):
        over_y = None
        for iy, offset_y in enumerate(OFFSETS):
            row = (3 * iy + iz) * chans_in
            part = jnp.dot(lhs[row:row + chans_in, :], rhs[:, pl.ds(at, size)], preferred_element_type=jnp.float32)
            part = shift_y(part, offset_y)
            over_y = part if over_y is None else over_y + part
        over_y = shift_z(over_y, offset_z)
        total = over_y if total is None else total + over_y
    out_ref[...] = total.astype(out_ref.dtype)


def backward(position, sources, blocks, halos, w, before, slab, out_dtype):
    number = len(blocks)
    chans, cells = blocks[0].shape
    chans_in = w.shape[1]
    size = cells // slab
    first = before is None
    whole = lambda a: pl.BlockSpec(a.shape, lambda n, s: (0,) * a.ndim, pipeline_mode=pl.Buffered(1))
    each = pl.BlockSpec((chans_in, size), lambda n, s: (0, n))
    args = (*halos, *blocks, w) + (() if first else (before,))
    return pl.pallas_call(
        functools.partial(backward_kernel, slab, sources, first),
        grid_spec=pltpu.PrefetchScalarGridSpec(
            num_scalar_prefetch=1, grid=(slab,),
            in_specs=[whole(a) for a in args[:2 * number + 1]] + ([] if first else [each]),
            out_specs=each,
            scratch_shapes=[pltpu.VMEM((9 * chans_in, 3 * number * chans), jnp.bfloat16),
                            pltpu.VMEM((3 * number * chans, cells), jnp.bfloat16)]),
        out_shape=jax.ShapeDtypeStruct((chans_in, cells), out_dtype),
        compiler_params=pltpu.CompilerParams(vmem_limit_bytes=VMEM_LIMIT),
        cost_estimate=pl.CostEstimate(flops=2*27*chans*chans_in*cells*number, bytes_accessed=w.size*2+chans_in*cells*4, transcendentals=0),
        name="backward",
    )(position, *args)


def padded(block, sides, width):
    for axis, dim in sides:
        count = lax.axis_size(axis)
        forward_ring = [(i, (i + 1) % count) for i in range(count)]
        backward_ring = [(target, source) for source, target in forward_ring]
        low = lax.ppermute(
            lax.slice_in_dim(block, block.shape[dim] - width, None, axis=dim), axis, forward_ring
        )
        high = lax.ppermute(lax.slice_in_dim(block, 0, width, axis=dim), axis, backward_ring)
        block = jnp.concatenate([low, block, high], axis=dim)
    return block


def stack_yz(block, rows_y):
    chans, slab_len, plane_size = block.shape
    shaped = block.reshape(chans, slab_len, rows_y, NZ)
    pieces = []
    for offset_y in OFFSETS:
        for offset_z in OFFSETS:
            pieces.append(jnp.roll(shaped, (-offset_y, -offset_z), axis=(2, 3)))
    return jnp.stack(pieces).reshape(9 * chans, slab_len * plane_size)


def general(inputs, weights, out_grad):
    chans_in, slab_len, plane_size = inputs.shape
    chans_out = out_grad.shape[0]
    full_out = weights.shape[2]
    rows_y = plane_size // NZ
    cell_count = slab_len * plane_size
    halo_in = padded(inputs, (("slab", 1),), 1)
    grad_all = lax.all_gather(out_grad, "chan", axis=0, tiled=True)
    halo_grad = padded(grad_all, (("slab", 1),), 1)
    running = jnp.zeros((full_out, cell_count), jnp.float32)
    for index_x, offset_x in enumerate(OFFSETS):
        columns = stack_yz(halo_in[:, 1 + offset_x : 1 + offset_x + slab_len], rows_y)
        weight_x = weights[9 * index_x : 9 * index_x + 9].reshape(9 * chans_in, full_out)
        running = running + lax.dot_general(
            weight_x, columns, (((0,), (0,)), ((), ())), preferred_element_type=jnp.float32
        )
    own_rows = lax.psum_scatter(running, "chan", scatter_dimension=0, tiled=True)
    conv_out = own_rows.astype(jnp.bfloat16).reshape(chans_out, slab_len, plane_size)
    running_grad = jnp.zeros((chans_in, slab_len, rows_y, NZ), jnp.float32)
    for index_x, offset_x in enumerate(OFFSETS):
        plane_x = halo_grad[:, 1 - offset_x : 1 - offset_x + slab_len].reshape(full_out, cell_count)
        weight_x = weights[9 * index_x : 9 * index_x + 9].reshape(9 * chans_in, full_out)
        product = lax.dot_general(
            weight_x, plane_x, (((1,), (0,)), ((), ())), preferred_element_type=jnp.float32
        )
        product = product.reshape(9, chans_in, slab_len, rows_y, NZ)
        for index_y, offset_y in enumerate(OFFSETS):
            for index_z, offset_z in enumerate(OFFSETS):
                running_grad = running_grad + jnp.roll(
                    product[3 * index_y + index_z], (offset_y, offset_z), axis=(2, 3)
                )
    input_grad = running_grad.reshape(chans_in, slab_len, plane_size).astype(jnp.bfloat16)
    return (conv_out, input_grad)


def edge_planes(block, size):
    count = lax.axis_size("slab")
    first, last = block[:, :size], block[:, block.shape[1] - size :]
    upward = [(i, (i + 1) % count) for i in range(count)]
    if count <= 2:
        return lax.ppermute(jnp.concatenate([last, first], axis=1), "slab", upward)
    downward = [(target, source) for source, target in upward]
    low, high = lax.ppermute(last, "slab", upward), lax.ppermute(first, "slab", downward)
    return jnp.concatenate([low, high], axis=1)


LINE = 4
TOP = 32768.0


def scale_of(marks):
    marks = marks.astype(jnp.float32)
    return sum(marks[2 * i : 2 * i + 1] * marks[2 * i + 1 : 2 * i + 2] for i in range(LINE))


def pack(total, marks):
    scaled = (total * (TOP / scale_of(marks))).astype(jnp.float16)
    return jnp.concatenate([scaled, marks], axis=0)


def unpack(parcel):
    rows = parcel.shape[0] - 2 * LINE
    return parcel[:rows].astype(jnp.float32) * (scale_of(parcel[rows:]) * (1.0 / TOP)), parcel[rows:]


def pack_sum(total, marks, parcel):
    other, other_marks = unpack(parcel)
    return pack(total + other, marks + other_marks)


def line_of_four(inputs, weights, out_grad):
    chans, slab_len, size = inputs.shape
    cells = slab_len * size
    place = lax.axis_index("chan")
    position = place.reshape(1)
    middle = (place == 1) | (place == 2)

    def move(block, pairs):
        return lax.ppermute(block, "chan", pairs)

    grad = out_grad.reshape(chans, cells)
    field = inputs.reshape(chans, cells)
    from_below = move(grad, [(0, 1), (1, 2), (2, 3)])
    from_above = move(grad, [(1, 0), (2, 1), (3, 2)])
    field_edges = edge_planes(field, size)
    grad_edges = edge_planes(grad, size)

    partial, marks = forward(position, field, field_edges, weights, slab_len)
    marks = marks.astype(jnp.float16)
    block = lambda index: lax.dynamic_slice_in_dim(partial, index * chans, chans, axis=0)

    sum_1 = move(pack(block(jnp.where(place < 2, 3, 0)), marks), [(0, 1), (3, 2)])
    below_2 = move(from_below, [(1, 2), (2, 3)])
    above_2 = move(from_above, [(2, 1), (1, 0)])
    second = jnp.where(place == 0, from_above, from_below)
    second_edges = edge_planes(second, size)
    grad_half = backward(
        position, (own_place, second_place), (grad, second), (grad_edges, second_edges),
        weights, None, slab_len, jnp.float32,
    )

    parcel = pack_sum(block((place + 2) % 4), marks, sum_1)
    sum_below = move(parcel, [(0, 1), (1, 2)])
    sum_above = move(parcel, [(3, 2), (2, 1)])
    from_above, below_2, above_2, grad_half = lax.optimization_barrier(
        (from_above, below_2, above_2, grad_half)
    )
    relayed = jnp.where(place >= 2, below_2, above_2)
    far = move(relayed, [(2, 3), (1, 0)])
    third = jnp.where(middle, from_above, relayed)
    fourth = jnp.where(middle, relayed, far)
    third_edges = edge_planes(third, size)
    fourth_edges = edge_planes(fourth, size)

    upward = pack_sum(block(jnp.minimum(place + 1, 3)), marks, sum_below)
    downward = pack_sum(block(jnp.maximum(place - 1, 0)), marks, sum_above)
    last_below = move(upward, [(0, 1), (1, 2), (2, 3)])
    last_above = move(downward, [(3, 2), (2, 1), (1, 0)])
    input_grad = backward(
        position, (third_place, fourth_place), (third, fourth), (third_edges, fourth_edges),
        weights, grad_half, slab_len, jnp.bfloat16,
    )
    conv_out = block(place) + unpack(last_below)[0] + unpack(last_above)[0]
    shape = (chans, slab_len, size)
    return conv_out.astype(jnp.bfloat16).reshape(shape), input_grad.reshape(shape)


def own_place(place):
    return place


def second_place(place):
    return jnp.where(place == 0, 1, place - 1)


def third_place(place):
    return jnp.where(place == 3, 1, jnp.where(place == 2, 3, 2))


def fourth_place(place):
    return jnp.where(place < 2, 3, 0)


def chosen(inputs, weights, out_grad):
    chans, size = inputs.shape[0], inputs.shape[2]
    line = lax.axis_size("chan") == 4 and weights.shape[2] == 4 * chans and out_grad.shape[0] == chans
    if line and chans % 128 == 0 and size % 128 == 0:
        return line_of_four(inputs, weights, out_grad)
    return general(inputs, weights, out_grad)


def solution(mesh):
    in_specs = (
        P(("batch", "chan"), "slab", None),
        P(None, "chan", None),
        P(("batch", "chan"), "slab", None),
    )
    out_specs = (P(("batch", "chan"), "slab", None), P(("batch", "chan"), "slab", None))
    return jax.shard_map(chosen, mesh=mesh, in_specs=in_specs, out_specs=out_specs, check_vma=False)
```

```python
import functools

import jax
import jax.numpy as jnp
from jax import lax
from jax.experimental import pallas as pl
from jax.experimental.pallas import tpu as pltpu
from jax.sharding import PartitionSpec as P


NZ = 64
OFFSETS = (-1, 0, 1)
FORWARD_VMEM = 28 * 2**20
BACKWARD_VMEM = 28 * 2**20


def shift_z(block, offset):
    if offset == 0:
        return block
    lanes = block.shape[1]
    z = lax.broadcasted_iota(jnp.int32, block.shape, 1) % NZ
    plain = pltpu.roll(block, offset % lanes, 1)
    wrapped = pltpu.roll(block, (offset - NZ * offset) % lanes, 1)
    edge = z == (0 if offset == 1 else NZ - 1)
    return jnp.where(edge, wrapped, plain)


def shift_y(block, offset):
    if offset == 0:
        return block
    return pltpu.roll(block, (NZ * offset) % block.shape[1], 1)


def forward_kernel(slab, position_ref, halo_ref, x_ref, w_ref, out_ref, marks_ref, columns, wt, top_ref):
    plane = pl.program_id(0)
    chans, size = w_ref.shape[1], out_ref.shape[1]

    @pl.when(plane == 0)
    def _():
        for o in range(27):
            wt[:, o * chans:(o + 1) * chans] = w_ref[o].T
        for p in range(slab + 2):
            if p == 0:
                source = halo_ref[:, :size]
            elif p == slab + 1:
                source = halo_ref[:, size:]
            else:
                source = x_ref[:, (p - 1) * size:p * size]
            for iz, offset_z in enumerate(OFFSETS):
                moved = shift_z(source, -offset_z)
                for iy, offset_y in enumerate(OFFSETS):
                    row = (3 * iy + iz) * chans
                    columns[row:row + chans, p * size:(p + 1) * size] = shift_y(moved, -offset_y)

    total = None
    for ix in range(3):
        at = pl.multiple_of((plane + ix) * size, size)
        part = jnp.dot(wt[:, ix * 9 * chans:(ix + 1) * 9 * chans], columns[:, pl.ds(at, size)],
                       preferred_element_type=jnp.float32)
        total = part if total is None else total + part
    out_ref[...] = total
    top = jnp.max(jnp.max(jnp.abs(total), axis=0, keepdims=True), axis=1, keepdims=True)
    top = jnp.broadcast_to(top, top_ref.shape)

    @pl.when(plane == 0)
    def _():
        top_ref[...] = top

    @pl.when(plane > 0)
    def _():
        top_ref[...] = jnp.maximum(top_ref[...], top)

    @pl.when(plane == slab - 1)
    def _():
        power = jnp.clip(jnp.ceil(jnp.log2(jnp.maximum(top_ref[...], 1e-30))), -28.0, 15.0)
        high = jnp.maximum(power, -14.0)
        row = lax.broadcasted_iota(jnp.int32, top_ref.shape, 0) - 2 * position_ref[0]
        mark = jnp.where(row == 0, jnp.exp2(high), jnp.where(row == 1, jnp.exp2(power - high), 0.0))
        marks_ref[...] = mark


def forward(position, x, halo, w, slab):
    chans, cells = x.shape
    size = cells // slab
    full = w.shape[2]
    whole = lambda a: pl.BlockSpec(a.shape, lambda n, s: (0,) * a.ndim, pipeline_mode=pl.Buffered(1))
    return pl.pallas_call(
        functools.partial(forward_kernel, slab),
        grid_spec=pltpu.PrefetchScalarGridSpec(
            num_scalar_prefetch=1,
            grid=(slab,),
            in_specs=[whole(halo), whole(x), whole(w)],
            out_specs=[
                pl.BlockSpec((full, size), lambda n, s: (0, n)),
                pl.BlockSpec((8, 128), lambda n, s: (0, 0)),
            ],
            scratch_shapes=[
                pltpu.VMEM((9 * chans, (slab + 2) * size), jnp.bfloat16),
                pltpu.VMEM((full, 27 * chans), jnp.bfloat16),
                pltpu.VMEM((8, 128), jnp.float32),
            ],
        ),
        out_shape=[
            jax.ShapeDtypeStruct((full, cells), jnp.float32),
            jax.ShapeDtypeStruct((8, 128), jnp.float32),
        ],
        compiler_params=pltpu.CompilerParams(vmem_limit_bytes=FORWARD_VMEM),
        cost_estimate=pl.CostEstimate(
            flops=2 * 27 * chans * full * cells,
            bytes_accessed=w.size * 2 + full * cells * 4,
            transcendentals=0,
        ),
        name="forward",
    )(position, halo, x, w)


def backward_kernel(slab, sources, first, position_ref, *refs):
    number = len(sources)
    halos, blocks = refs[:number], refs[number:2 * number]
    w_ref = refs[2 * number]
    before = None if first else refs[2 * number + 1]
    out_ref, lhs, rhs = refs[-3:]
    plane = pl.program_id(0)
    chans_in, size = w_ref.shape[1], out_ref.shape[1]
    chans = blocks[0].shape[0]

    @pl.when(plane == 0)
    def _():
        for k in range(number):
            at = pl.multiple_of(sources[k](position_ref[0]) * chans, chans)
            for ix, offset_x in enumerate(OFFSETS):
                row = (3 * k + ix) * chans
                for o in range(9):
                    lhs[o * chans_in:(o + 1) * chans_in, row:row + chans] = w_ref[9 * ix + o, :, pl.ds(at, chans)]
                if offset_x == 0:
                    rhs[row:row + chans, :] = blocks[k][...]
                elif offset_x == 1:
                    rhs[row:row + chans, :size] = halos[k][:, :size]
                    rhs[row:row + chans, size:] = blocks[k][:, :(slab - 1) * size]
                else:
                    rhs[row:row + chans, :(slab - 1) * size] = blocks[k][:, size:]
                    rhs[row:row + chans, (slab - 1) * size:] = halos[k][:, size:]

    at = pl.multiple_of(plane * size, size)
    total = None if first else before[...]
    for iz, offset_z in enumerate(OFFSETS):
        over_y = None
        for iy, offset_y in enumerate(OFFSETS):
            row = (3 * iy + iz) * chans_in
            part = jnp.dot(lhs[row:row + chans_in, :], rhs[:, pl.ds(at, size)], preferred_element_type=jnp.float32)
            part = shift_y(part, offset_y)
            over_y = part if over_y is None else over_y + part
        over_y = shift_z(over_y, offset_z)
        total = over_y if total is None else total + over_y
    out_ref[...] = total.astype(out_ref.dtype)


def backward(position, sources, blocks, halos, w, before, slab, out_dtype):
    number = len(blocks)
    chans, cells = blocks[0].shape
    chans_in = w.shape[1]
    size = cells // slab
    first = before is None
    whole = lambda a: pl.BlockSpec(a.shape, lambda n, s: (0,) * a.ndim, pipeline_mode=pl.Buffered(1))
    each = pl.BlockSpec((chans_in, size), lambda n, s: (0, n))
    args = (*halos, *blocks, w) + (() if first else (before,))
    return pl.pallas_call(
        functools.partial(backward_kernel, slab, sources, first),
        grid_spec=pltpu.PrefetchScalarGridSpec(
            num_scalar_prefetch=1, grid=(slab,),
            in_specs=[whole(a) for a in args[:2 * number + 1]] + ([] if first else [each]),
            out_specs=each,
            scratch_shapes=[pltpu.VMEM((9 * chans_in, 3 * number * chans), jnp.bfloat16),
                            pltpu.VMEM((3 * number * chans, cells), jnp.bfloat16)]),
        out_shape=jax.ShapeDtypeStruct((chans_in, cells), out_dtype),
        compiler_params=pltpu.CompilerParams(vmem_limit_bytes=BACKWARD_VMEM),
        cost_estimate=pl.CostEstimate(flops=2*27*chans*chans_in*cells*number, bytes_accessed=w.size*2+chans_in*cells*4, transcendentals=0),
        name="backward",
    )(position, *args)


def padded(block, sides, width):
    for axis, dim in sides:
        count = lax.axis_size(axis)
        forward_ring = [(i, (i + 1) % count) for i in range(count)]
        backward_ring = [(target, source) for source, target in forward_ring]
        low = lax.ppermute(
            lax.slice_in_dim(block, block.shape[dim] - width, None, axis=dim), axis, forward_ring
        )
        high = lax.ppermute(lax.slice_in_dim(block, 0, width, axis=dim), axis, backward_ring)
        block = jnp.concatenate([low, block, high], axis=dim)
    return block


def stack_yz(block, rows_y):
    chans, slab_len, plane_size = block.shape
    shaped = block.reshape(chans, slab_len, rows_y, NZ)
    pieces = []
    for offset_y in OFFSETS:
        for offset_z in OFFSETS:
            pieces.append(jnp.roll(shaped, (-offset_y, -offset_z), axis=(2, 3)))
    return jnp.stack(pieces).reshape(9 * chans, slab_len * plane_size)


def general(inputs, weights, out_grad):
    chans_in, slab_len, plane_size = inputs.shape
    chans_out = out_grad.shape[0]
    full_out = weights.shape[2]
    rows_y = plane_size // NZ
    cell_count = slab_len * plane_size
    halo_in = padded(inputs, (("slab", 1),), 1)
    grad_all = lax.all_gather(out_grad, "chan", axis=0, tiled=True)
    halo_grad = padded(grad_all, (("slab", 1),), 1)
    running = jnp.zeros((full_out, cell_count), jnp.float32)
    for index_x, offset_x in enumerate(OFFSETS):
        columns = stack_yz(halo_in[:, 1 + offset_x : 1 + offset_x + slab_len], rows_y)
        weight_x = weights[9 * index_x : 9 * index_x + 9].reshape(9 * chans_in, full_out)
        running = running + lax.dot_general(
            weight_x, columns, (((0,), (0,)), ((), ())), preferred_element_type=jnp.float32
        )
    own_rows = lax.psum_scatter(running, "chan", scatter_dimension=0, tiled=True)
    conv_out = own_rows.astype(jnp.bfloat16).reshape(chans_out, slab_len, plane_size)
    running_grad = jnp.zeros((chans_in, slab_len, rows_y, NZ), jnp.float32)
    for index_x, offset_x in enumerate(OFFSETS):
        plane_x = halo_grad[:, 1 - offset_x : 1 - offset_x + slab_len].reshape(full_out, cell_count)
        weight_x = weights[9 * index_x : 9 * index_x + 9].reshape(9 * chans_in, full_out)
        product = lax.dot_general(
            weight_x, plane_x, (((1,), (0,)), ((), ())), preferred_element_type=jnp.float32
        )
        product = product.reshape(9, chans_in, slab_len, rows_y, NZ)
        for index_y, offset_y in enumerate(OFFSETS):
            for index_z, offset_z in enumerate(OFFSETS):
                running_grad = running_grad + jnp.roll(
                    product[3 * index_y + index_z], (offset_y, offset_z), axis=(2, 3)
                )
    input_grad = running_grad.reshape(chans_in, slab_len, plane_size).astype(jnp.bfloat16)
    return (conv_out, input_grad)


def edge_planes(block, size):
    count = lax.axis_size("slab")
    first, last = block[:, :size], block[:, block.shape[1] - size :]
    upward = [(i, (i + 1) % count) for i in range(count)]
    if count <= 2:
        return lax.ppermute(jnp.concatenate([last, first], axis=1), "slab", upward)
    downward = [(target, source) for source, target in upward]
    low, high = lax.ppermute(last, "slab", upward), lax.ppermute(first, "slab", downward)
    return jnp.concatenate([low, high], axis=1)


LINE = 4
TOP = 32768.0
ROWS, LANES = 8, 128


def tiles(block):
    rows, columns = block.shape
    split = block.reshape(rows // ROWS, ROWS, columns // LANES, LANES)
    return split.transpose(0, 2, 1, 3).reshape(-1, LANES)


def untiled(block, rows):
    split = block.reshape(rows // ROWS, -1, ROWS, LANES)
    return split.transpose(0, 2, 1, 3).reshape(rows, -1)


def scale_of(marks):
    marks = marks.astype(jnp.float32)
    return sum(marks[2 * i : 2 * i + 1] * marks[2 * i + 1 : 2 * i + 2] for i in range(LINE))


def pack(total, marks):
    scaled = (total * (TOP / scale_of(marks))).astype(jnp.float16)
    return jnp.concatenate([scaled, marks], axis=0)


def unpack(parcel):
    return parcel[:-ROWS].astype(jnp.float32) * (scale_of(parcel[-ROWS:]) * (1.0 / TOP))


def line_of_four(inputs, weights, out_grad):
    chans, slab_len, size = inputs.shape
    cells = slab_len * size
    slabs = lax.axis_size("slab")
    place = lax.axis_index("chan")
    position = place.reshape(1)
    inner = (place == 1) | (place == 2)

    def swap_ends(block):
        return lax.ppermute(block, "chan", [(0, 1), (1, 0), (2, 3), (3, 2)])

    def swap_middle(block):
        pairs = []
        for slab in range(slabs):
            other = (slab + 1) % slabs
            pairs += [(slabs + slab, 2 * slabs + slab), (2 * slabs + slab, slabs + slab)]
            pairs += [(end * slabs + slab, end * slabs + other) for end in (0, 3)]
        return lax.ppermute(block, ("chan", "slab"), pairs)

    def block(index):
        return lax.dynamic_index_in_dim(partial, index, axis=0, keepdims=False)

    def partial_or_cotangent(index, cotangent):
        cotangent = tiles(cotangent).astype(jnp.float32)
        bound = jnp.maximum(jnp.max(jnp.abs(cotangent), axis=0, keepdims=True) * 1.01, 2.0**-14)
        row = lax.broadcasted_iota(jnp.int32, marks.shape, 0)
        bounds = jnp.where(row == 0, bound, jnp.where(row == 1, 1.0, 0.0)).astype(jnp.float16)
        return pack(jnp.where(inner, cotangent, block(index)), jnp.where(inner, bounds, marks))

    def sum_with(index, parcel, counts=True):
        others = jnp.where(counts, parcel[-ROWS:], jnp.zeros_like(marks))
        theirs = parcel[:-ROWS].astype(jnp.float32) * (scale_of(others) * (1.0 / TOP))
        return pack(block(index) + theirs, marks + others)

    def cotangent_of(parcel):
        return untiled(unpack(parcel).astype(jnp.bfloat16), chans)

    grad = out_grad.reshape(chans, cells)
    field = inputs.reshape(chans, cells)
    ends_1 = swap_ends(grad)
    middle_1 = swap_middle(grad)
    field_edges = edge_planes(field, size)
    grad_edges = edge_planes(grad, size)

    partial, marks = forward(position, field, field_edges, weights, slab_len)
    partial = tiles(partial).reshape(LINE, -1, LANES)
    marks = marks.astype(jnp.float16)

    middle_2 = swap_middle(ends_1)
    ends_2 = swap_ends(partial_or_cotangent(jnp.where(place < 2, 3, 0), middle_1))
    second_edges = edge_planes(ends_1, size)
    grad_half = backward(
        position, (own_place, second_place), (grad, ends_1), (grad_edges, second_edges),
        weights, None, slab_len, jnp.float32,
    )

    ends_3 = swap_ends(partial_or_cotangent(jnp.where(place < 2, 2, 1), middle_2))
    middle_3 = swap_middle(sum_with(jnp.where(place < 2, 3, 0), ends_2))
    third = jnp.where(inner, middle_1, cotangent_of(ends_2))
    third_edges = edge_planes(third, size)

    ends_4 = swap_ends(sum_with(place ^ 1, middle_3, inner))
    middle_4 = swap_middle(sum_with(jnp.where(place < 2, 2, 1), ends_3))
    fourth = jnp.where(inner, middle_2, cotangent_of(ends_3))
    fourth_edges = edge_planes(fourth, size)
    input_grad = backward(
        position, (third_place, fourth_place), (third, fourth), (third_edges, fourth_edges),
        weights, grad_half, slab_len, jnp.bfloat16,
    )
    conv_out = block(place) + unpack(ends_4) + jnp.where(inner, unpack(middle_4), 0.0)
    conv_out = untiled(conv_out.astype(jnp.bfloat16), chans)
    shape = (chans, slab_len, size)
    return conv_out.reshape(shape), input_grad.reshape(shape)


def own_place(place):
    return place


def second_place(place):
    return place ^ 1


def third_place(place):
    return jnp.where(place < 2, 2, 1)


def fourth_place(place):
    return jnp.where(place < 2, 3, 0)


def chosen(inputs, weights, out_grad):
    chans, size = inputs.shape[0], inputs.shape[2]
    line = lax.axis_size("chan") == 4 and weights.shape[2] == 4 * chans and out_grad.shape[0] == chans
    if line and chans % 128 == 0 and size % 128 == 0:
        return line_of_four(inputs, weights, out_grad)
    return general(inputs, weights, out_grad)


def solution(mesh):
    in_specs = (
        P(("batch", "chan"), "slab", None),
        P(None, "chan", None),
        P(("batch", "chan"), "slab", None),
    )
    out_specs = (P(("batch", "chan"), "slab", None), P(("batch", "chan"), "slab", None))
    return jax.shard_map(chosen, mesh=mesh, in_specs=in_specs, out_specs=out_specs, check_vma=False)
```

```python
import functools

import jax
import jax.numpy as jnp
from jax import lax
from jax.experimental import pallas as pl
from jax.experimental.pallas import tpu as pltpu
from jax.sharding import PartitionSpec as P


NZ = 64
OFFSETS = (-1, 0, 1)
FORWARD_VMEM = 28 * 2**20
BACKWARD_VMEM = 28 * 2**20


def shift_z(block, offset):
    if offset == 0:
        return block
    lanes = block.shape[1]
    z = lax.broadcasted_iota(jnp.int32, block.shape, 1) % NZ
    plain = pltpu.roll(block, offset % lanes, 1)
    wrapped = pltpu.roll(block, (offset - NZ * offset) % lanes, 1)
    edge = z == (0 if offset == 1 else NZ - 1)
    return jnp.where(edge, wrapped, plain)


def shift_y(block, offset):
    if offset == 0:
        return block
    return pltpu.roll(block, (NZ * offset) % block.shape[1], 1)


def forward_kernel(slab, sums, position_ref, halo_ref, x_ref, w_ref, *refs):
    out_refs, (marks_ref, columns, wt, top_ref) = refs[: len(sums)], refs[len(sums) :]
    plane = pl.program_id(0)
    chans, size = out_refs[0].shape

    @pl.when(plane == 0)
    def _():
        for i, place in enumerate(sums):
            at = pl.multiple_of(place(position_ref[0]) * chans, chans)
            for o in range(27):
                wt[i * chans:(i + 1) * chans, o * chans:(o + 1) * chans] = w_ref[o, :, pl.ds(at, chans)].T
        for p in range(slab + 2):
            if p == 0:
                source = halo_ref[:, :size]
            elif p == slab + 1:
                source = halo_ref[:, size:]
            else:
                source = x_ref[:, (p - 1) * size:p * size]
            for iz, offset_z in enumerate(OFFSETS):
                moved = shift_z(source, -offset_z)
                for iy, offset_y in enumerate(OFFSETS):
                    row = (3 * iy + iz) * chans
                    columns[row:row + chans, p * size:(p + 1) * size] = shift_y(moved, -offset_y)

    total = None
    for ix in range(3):
        at = pl.multiple_of((plane + ix) * size, size)
        part = jnp.dot(wt[:, ix * 9 * chans:(ix + 1) * 9 * chans], columns[:, pl.ds(at, size)],
                       preferred_element_type=jnp.float32)
        total = part if total is None else total + part
    for i, out_ref in enumerate(out_refs):
        out_ref[...] = total[i * chans:(i + 1) * chans]
    top = jnp.max(jnp.max(jnp.abs(total), axis=0, keepdims=True), axis=1, keepdims=True)
    top = jnp.broadcast_to(top, top_ref.shape)

    @pl.when(plane == 0)
    def _():
        top_ref[...] = top

    @pl.when(plane > 0)
    def _():
        top_ref[...] = jnp.maximum(top_ref[...], top)

    @pl.when(plane == slab - 1)
    def _():
        power = jnp.clip(jnp.ceil(jnp.log2(jnp.maximum(top_ref[...], 1e-30))), -28.0, 15.0)
        high = jnp.maximum(power, -14.0)
        row = lax.broadcasted_iota(jnp.int32, top_ref.shape, 0) - 2 * position_ref[0]
        mark = jnp.where(row == 0, jnp.exp2(high), jnp.where(row == 1, jnp.exp2(power - high), 0.0))
        marks_ref[...] = mark


def forward(position, sums, x, halo, w, slab):
    chans, cells = x.shape
    number, size = len(sums), cells // slab
    whole = lambda a: pl.BlockSpec(a.shape, lambda n, s: (0,) * a.ndim, pipeline_mode=pl.Buffered(1))
    each = pl.BlockSpec((chans, size), lambda n, s: (0, n))
    outs = [jax.ShapeDtypeStruct((chans, cells), jnp.float32)] * number
    outs.append(jax.ShapeDtypeStruct((8, 128), jnp.float32))
    *partials, marks = pl.pallas_call(
        functools.partial(forward_kernel, slab, sums),
        grid_spec=pltpu.PrefetchScalarGridSpec(
            num_scalar_prefetch=1,
            grid=(slab,),
            in_specs=[whole(halo), whole(x), whole(w)],
            out_specs=[each] * number + [pl.BlockSpec((8, 128), lambda n, s: (0, 0))],
            scratch_shapes=[
                pltpu.VMEM((9 * chans, (slab + 2) * size), jnp.bfloat16),
                pltpu.VMEM((number * chans, 27 * chans), jnp.bfloat16),
                pltpu.VMEM((8, 128), jnp.float32),
            ],
        ),
        out_shape=outs,
        compiler_params=pltpu.CompilerParams(vmem_limit_bytes=FORWARD_VMEM),
        cost_estimate=pl.CostEstimate(
            flops=2 * 27 * chans * chans * number * cells,
            bytes_accessed=w.size * 2 + number * chans * cells * 4,
            transcendentals=0,
        ),
        name="forward",
    )(position, halo, x, w)
    return partials, marks


def backward_kernel(slab, sources, first, position_ref, *refs):
    number = len(sources)
    halos, blocks = refs[:number], refs[number:2 * number]
    w_ref = refs[2 * number]
    before = None if first else refs[2 * number + 1]
    out_ref, lhs, rhs = refs[-3:]
    plane = pl.program_id(0)
    chans_in, size = w_ref.shape[1], out_ref.shape[1]
    chans = blocks[0].shape[0]

    @pl.when(plane == 0)
    def _():
        for k in range(number):
            at = pl.multiple_of(sources[k](position_ref[0]) * chans, chans)
            for ix, offset_x in enumerate(OFFSETS):
                row = (3 * k + ix) * chans
                for o in range(9):
                    lhs[o * chans_in:(o + 1) * chans_in, row:row + chans] = w_ref[9 * ix + o, :, pl.ds(at, chans)]
                if offset_x == 0:
                    rhs[row:row + chans, :] = blocks[k][...]
                elif offset_x == 1:
                    rhs[row:row + chans, :size] = halos[k][:, :size]
                    rhs[row:row + chans, size:] = blocks[k][:, :(slab - 1) * size]
                else:
                    rhs[row:row + chans, :(slab - 1) * size] = blocks[k][:, size:]
                    rhs[row:row + chans, (slab - 1) * size:] = halos[k][:, size:]

    at = pl.multiple_of(plane * size, size)
    total = None if first else before[...]
    for iz, offset_z in enumerate(OFFSETS):
        over_y = None
        for iy, offset_y in enumerate(OFFSETS):
            row = (3 * iy + iz) * chans_in
            part = jnp.dot(lhs[row:row + chans_in, :], rhs[:, pl.ds(at, size)], preferred_element_type=jnp.float32)
            part = shift_y(part, offset_y)
            over_y = part if over_y is None else over_y + part
        over_y = shift_z(over_y, offset_z)
        total = over_y if total is None else total + over_y
    out_ref[...] = total.astype(out_ref.dtype)


def backward(position, sources, blocks, halos, w, before, slab, out_dtype):
    number = len(blocks)
    chans, cells = blocks[0].shape
    chans_in = w.shape[1]
    size = cells // slab
    first = before is None
    whole = lambda a: pl.BlockSpec(a.shape, lambda n, s: (0,) * a.ndim, pipeline_mode=pl.Buffered(1))
    each = pl.BlockSpec((chans_in, size), lambda n, s: (0, n))
    args = (*halos, *blocks, w) + (() if first else (before,))
    return pl.pallas_call(
        functools.partial(backward_kernel, slab, sources, first),
        grid_spec=pltpu.PrefetchScalarGridSpec(
            num_scalar_prefetch=1, grid=(slab,),
            in_specs=[whole(a) for a in args[:2 * number + 1]] + ([] if first else [each]),
            out_specs=each,
            scratch_shapes=[pltpu.VMEM((9 * chans_in, 3 * number * chans), jnp.bfloat16),
                            pltpu.VMEM((3 * number * chans, cells), jnp.bfloat16)]),
        out_shape=jax.ShapeDtypeStruct((chans_in, cells), out_dtype),
        compiler_params=pltpu.CompilerParams(vmem_limit_bytes=BACKWARD_VMEM),
        cost_estimate=pl.CostEstimate(flops=2*27*chans*chans_in*cells*number, bytes_accessed=w.size*2+chans_in*cells*4, transcendentals=0),
        name="backward",
    )(position, *args)


def padded(block, sides, width):
    for axis, dim in sides:
        count = lax.axis_size(axis)
        forward_ring = [(i, (i + 1) % count) for i in range(count)]
        backward_ring = [(target, source) for source, target in forward_ring]
        low = lax.ppermute(
            lax.slice_in_dim(block, block.shape[dim] - width, None, axis=dim), axis, forward_ring
        )
        high = lax.ppermute(lax.slice_in_dim(block, 0, width, axis=dim), axis, backward_ring)
        block = jnp.concatenate([low, block, high], axis=dim)
    return block


def stack_yz(block, rows_y):
    chans, slab_len, plane_size = block.shape
    shaped = block.reshape(chans, slab_len, rows_y, NZ)
    pieces = []
    for offset_y in OFFSETS:
        for offset_z in OFFSETS:
            pieces.append(jnp.roll(shaped, (-offset_y, -offset_z), axis=(2, 3)))
    return jnp.stack(pieces).reshape(9 * chans, slab_len * plane_size)


def general(inputs, weights, out_grad):
    chans_in, slab_len, plane_size = inputs.shape
    chans_out = out_grad.shape[0]
    full_out = weights.shape[2]
    rows_y = plane_size // NZ
    cell_count = slab_len * plane_size
    halo_in = padded(inputs, (("slab", 1),), 1)
    grad_all = lax.all_gather(out_grad, "chan", axis=0, tiled=True)
    halo_grad = padded(grad_all, (("slab", 1),), 1)
    running = jnp.zeros((full_out, cell_count), jnp.float32)
    for index_x, offset_x in enumerate(OFFSETS):
        columns = stack_yz(halo_in[:, 1 + offset_x : 1 + offset_x + slab_len], rows_y)
        weight_x = weights[9 * index_x : 9 * index_x + 9].reshape(9 * chans_in, full_out)
        running = running + lax.dot_general(
            weight_x, columns, (((0,), (0,)), ((), ())), preferred_element_type=jnp.float32
        )
    own_rows = lax.psum_scatter(running, "chan", scatter_dimension=0, tiled=True)
    conv_out = own_rows.astype(jnp.bfloat16).reshape(chans_out, slab_len, plane_size)
    running_grad = jnp.zeros((chans_in, slab_len, rows_y, NZ), jnp.float32)
    for index_x, offset_x in enumerate(OFFSETS):
        plane_x = halo_grad[:, 1 - offset_x : 1 - offset_x + slab_len].reshape(full_out, cell_count)
        weight_x = weights[9 * index_x : 9 * index_x + 9].reshape(9 * chans_in, full_out)
        product = lax.dot_general(
            weight_x, plane_x, (((1,), (0,)), ((), ())), preferred_element_type=jnp.float32
        )
        product = product.reshape(9, chans_in, slab_len, rows_y, NZ)
        for index_y, offset_y in enumerate(OFFSETS):
            for index_z, offset_z in enumerate(OFFSETS):
                running_grad = running_grad + jnp.roll(
                    product[3 * index_y + index_z], (offset_y, offset_z), axis=(2, 3)
                )
    input_grad = running_grad.reshape(chans_in, slab_len, plane_size).astype(jnp.bfloat16)
    return (conv_out, input_grad)


def edge_planes(block, size):
    count = lax.axis_size("slab")
    first, last = block[:, :size], block[:, block.shape[1] - size :]
    upward = [(i, (i + 1) % count) for i in range(count)]
    if count <= 2:
        return lax.ppermute(jnp.concatenate([last, first], axis=1), "slab", upward)
    downward = [(target, source) for source, target in upward]
    low, high = lax.ppermute(last, "slab", upward), lax.ppermute(first, "slab", downward)
    return jnp.concatenate([low, high], axis=1)


LINE = 4
TOP = 32768.0
ROWS, LANES = 8, 128


def tiles(block):
    rows, columns = block.shape
    split = block.reshape(rows // ROWS, ROWS, columns // LANES, LANES)
    return split.transpose(0, 2, 1, 3).reshape(-1, LANES)


def untiled(block, rows):
    split = block.reshape(rows // ROWS, -1, ROWS, LANES)
    return split.transpose(0, 2, 1, 3).reshape(rows, -1)


def scale_of(marks):
    marks = marks.astype(jnp.float32)
    return sum(marks[2 * i : 2 * i + 1] * marks[2 * i + 1 : 2 * i + 2] for i in range(LINE))


def pack(total, marks):
    scaled = (total * (TOP / scale_of(marks))).astype(jnp.float16)
    return jnp.concatenate([scaled, marks], axis=0)


def unpack(parcel):
    return parcel[:-ROWS].astype(jnp.float32) * (scale_of(parcel[-ROWS:]) * (1.0 / TOP))


def line_of_four(inputs, weights, out_grad):
    shape = inputs.shape
    chans, slab_len, size = shape
    slabs = lax.axis_size("slab")
    place = lax.axis_index("chan")
    position = place.reshape(1)
    inner = (place == 1) | (place == 2)

    def swap_ends(block):
        return lax.ppermute(block, "chan", [(0, 1), (1, 0), (2, 3), (3, 2)])

    def swap_middle(block):
        pairs = []
        for slab in range(slabs):
            other = (slab + 1) % slabs
            pairs += [(slabs + slab, 2 * slabs + slab), (2 * slabs + slab, slabs + slab)]
            pairs += [(end * slabs + slab, end * slabs + other) for end in (0, 3)]
        return lax.ppermute(block, ("chan", "slab"), pairs)

    def partial_or_cotangent(partial, marks, cotangent):
        cotangent = tiles(cotangent).astype(jnp.float32)
        bound = jnp.maximum(jnp.max(jnp.abs(cotangent), axis=0, keepdims=True) * 1.01, 2.0**-14)
        row = lax.broadcasted_iota(jnp.int32, marks.shape, 0)
        bounds = jnp.where(row == 0, bound, jnp.where(row == 1, 1.0, 0.0)).astype(jnp.float16)
        return pack(jnp.where(inner, cotangent, partial), jnp.where(inner, bounds, marks))

    def sum_with(partial, marks, parcel, counts=True):
        others = jnp.where(counts, parcel[-ROWS:], jnp.zeros_like(marks))
        theirs = parcel[:-ROWS].astype(jnp.float32) * (scale_of(others) * (1.0 / TOP))
        return pack(partial + theirs, marks + others)

    def cotangent_of(parcel):
        return untiled(unpack(parcel).astype(jnp.bfloat16), chans)

    grad = out_grad.reshape(chans, slab_len * size)
    field = inputs.reshape(chans, slab_len * size)
    ends_1 = swap_ends(grad)
    middle_1 = swap_middle(grad)
    field_edges = edge_planes(field, size)
    grad_edges = edge_planes(grad, size)
    (first,), first_marks = forward(position, (first_sum,), field, field_edges, weights, slab_len)
    first = tiles(first)
    first_marks = first_marks.astype(jnp.float16)

    middle_2 = swap_middle(ends_1)
    parcel = partial_or_cotangent(first, first_marks, middle_1)
    parcel, position_2 = lax.optimization_barrier((parcel, position))
    ends_2 = swap_ends(parcel)
    second_edges = edge_planes(ends_1, size)
    partials, marks = forward(
        position_2, (second_sum, third_sum, own_place), field, field_edges, weights, slab_len
    )
    second, third, own = (tiles(partial) for partial in partials)
    marks = marks.astype(jnp.float16)

    ends_3 = swap_ends(partial_or_cotangent(second, marks, middle_2))
    middle_3 = swap_middle(sum_with(first, first_marks, ends_2))
    grad_half = backward(
        position, (own_place, second_place), (grad, ends_1), (grad_edges, second_edges),
        weights, None, slab_len, jnp.float32,
    )
    grad_2 = jnp.where(inner, middle_1, cotangent_of(ends_2))
    edges_2 = edge_planes(grad_2, size)

    ends_4 = swap_ends(sum_with(third, marks, middle_3, inner))
    middle_4 = swap_middle(sum_with(second, marks, ends_3))
    grad_3 = jnp.where(inner, middle_2, cotangent_of(ends_3))
    edges_3 = edge_planes(grad_3, size)
    input_grad = backward(
        position, (third_place, fourth_place), (grad_2, grad_3), (edges_2, edges_3),
        weights, grad_half, slab_len, jnp.bfloat16,
    )
    conv_out = own + unpack(ends_4) + jnp.where(inner, unpack(middle_4), 0.0)
    conv_out = untiled(conv_out.astype(jnp.bfloat16), chans)
    return conv_out.reshape(shape), input_grad.reshape(shape)


def first_sum(place):
    return jnp.where(place < 2, 3, 0)


def second_sum(place):
    return jnp.where(place < 2, 2, 1)


def third_sum(place):
    return place ^ 1


def own_place(place):
    return place


def second_place(place):
    return place ^ 1


def third_place(place):
    return jnp.where(place < 2, 2, 1)


def fourth_place(place):
    return jnp.where(place < 2, 3, 0)


def chosen(inputs, weights, out_grad):
    chans, size = inputs.shape[0], inputs.shape[2]
    line = lax.axis_size("chan") == 4 and weights.shape[2] == 4 * chans and out_grad.shape[0] == chans
    if line and chans % 128 == 0 and size % 128 == 0:
        return line_of_four(inputs, weights, out_grad)
    return general(inputs, weights, out_grad)


def solution(mesh):
    in_specs = (
        P(("batch", "chan"), "slab", None),
        P(None, "chan", None),
        P(("batch", "chan"), "slab", None),
    )
    out_specs = (P(("batch", "chan"), "slab", None), P(("batch", "chan"), "slab", None))
    return jax.shard_map(chosen, mesh=mesh, in_specs=in_specs, out_specs=out_specs, check_vma=False)
```

```python
import functools

import jax
import jax.numpy as jnp
from jax import lax
from jax.experimental import pallas as pl
from jax.experimental.pallas import tpu as pltpu
from jax.sharding import PartitionSpec as P


NZ = 64
OFFSETS = (-1, 0, 1)
FORWARD_VMEM = 28 * 2**20
BACKWARD_VMEM = 28 * 2**20


def shift_z(block, offset):
    if offset == 0:
        return block
    lanes = block.shape[1]
    z = lax.broadcasted_iota(jnp.int32, block.shape, 1) % NZ
    plain = pltpu.roll(block, offset % lanes, 1)
    wrapped = pltpu.roll(block, (offset - NZ * offset) % lanes, 1)
    edge = z == (0 if offset == 1 else NZ - 1)
    return jnp.where(edge, wrapped, plain)


def shift_y(block, offset):
    if offset == 0:
        return block
    return pltpu.roll(block, (NZ * offset) % block.shape[1], 1)


def forward_kernel(slab, sums, position_ref, halo_ref, x_ref, w_ref, *refs):
    out_refs, (marks_ref, columns, wt, top_ref) = refs[: len(sums)], refs[len(sums) :]
    plane = pl.program_id(0)
    chans, size = out_refs[0].shape

    @pl.when(plane == 0)
    def _():
        for i, place in enumerate(sums):
            at = pl.multiple_of(place(position_ref[0]) * chans, chans)
            for o in range(27):
                wt[i * chans:(i + 1) * chans, o * chans:(o + 1) * chans] = w_ref[o, :, pl.ds(at, chans)].T
        for p in range(slab + 2):
            if p == 0:
                source = halo_ref[:, :size]
            elif p == slab + 1:
                source = halo_ref[:, size:]
            else:
                source = x_ref[:, (p - 1) * size:p * size]
            for iz, offset_z in enumerate(OFFSETS):
                moved = shift_z(source, -offset_z)
                for iy, offset_y in enumerate(OFFSETS):
                    row = (3 * iy + iz) * chans
                    columns[row:row + chans, p * size:(p + 1) * size] = shift_y(moved, -offset_y)

    total = None
    for ix in range(3):
        at = pl.multiple_of((plane + ix) * size, size)
        part = jnp.dot(wt[:, ix * 9 * chans:(ix + 1) * 9 * chans], columns[:, pl.ds(at, size)],
                       preferred_element_type=jnp.float32)
        total = part if total is None else total + part
    for i, out_ref in enumerate(out_refs):
        out_ref[...] = total[i * chans:(i + 1) * chans]
    top = jnp.max(jnp.max(jnp.abs(total), axis=0, keepdims=True), axis=1, keepdims=True)
    top = jnp.broadcast_to(top, top_ref.shape)

    @pl.when(plane == 0)
    def _():
        top_ref[...] = top

    @pl.when(plane > 0)
    def _():
        top_ref[...] = jnp.maximum(top_ref[...], top)

    @pl.when(plane == slab - 1)
    def _():
        power = jnp.clip(jnp.ceil(jnp.log2(jnp.maximum(top_ref[...], 1e-30))), -28.0, 15.0)
        high = jnp.maximum(power, -14.0)
        row = lax.broadcasted_iota(jnp.int32, top_ref.shape, 0) - 2 * position_ref[0]
        mark = jnp.where(row == 0, jnp.exp2(high), jnp.where(row == 1, jnp.exp2(power - high), 0.0))
        marks_ref[...] = mark


def forward(position, sums, x, halo, w, slab):
    chans, cells = x.shape
    number, size = len(sums), cells // slab
    whole = lambda a: pl.BlockSpec(a.shape, lambda n, s: (0,) * a.ndim, pipeline_mode=pl.Buffered(1))
    each = pl.BlockSpec((chans, size), lambda n, s: (0, n))
    outs = [jax.ShapeDtypeStruct((chans, cells), jnp.float32)] * number
    outs.append(jax.ShapeDtypeStruct((8, 128), jnp.float32))
    *partials, marks = pl.pallas_call(
        functools.partial(forward_kernel, slab, sums),
        grid_spec=pltpu.PrefetchScalarGridSpec(
            num_scalar_prefetch=1,
            grid=(slab,),
            in_specs=[whole(halo), whole(x), whole(w)],
            out_specs=[each] * number + [pl.BlockSpec((8, 128), lambda n, s: (0, 0))],
            scratch_shapes=[
                pltpu.VMEM((9 * chans, (slab + 2) * size), jnp.bfloat16),
                pltpu.VMEM((number * chans, 27 * chans), jnp.bfloat16),
                pltpu.VMEM((8, 128), jnp.float32),
            ],
        ),
        out_shape=outs,
        compiler_params=pltpu.CompilerParams(vmem_limit_bytes=FORWARD_VMEM),
        cost_estimate=pl.CostEstimate(
            flops=2 * 27 * chans * chans * number * cells,
            bytes_accessed=w.size * 2 + number * chans * cells * 4,
            transcendentals=0,
        ),
        name="forward",
    )(position, halo, x, w)
    return partials, marks


def backward_kernel(slab, sources, first, position_ref, *refs):
    number = len(sources)
    halos, blocks = refs[:number], refs[number:2 * number]
    w_ref = refs[2 * number]
    before = None if first else refs[2 * number + 1]
    out_ref, lhs, rhs = refs[-3:]
    plane = pl.program_id(0)
    chans_in, size = w_ref.shape[1], blocks[0].shape[1] // slab
    chans = blocks[0].shape[0]

    @pl.when(plane == 0)
    def _():
        for k in range(number):
            at = pl.multiple_of(sources[k](position_ref[0]) * chans, chans)
            for ix, offset_x in enumerate(OFFSETS):
                row = (3 * k + ix) * chans
                for o in range(9):
                    lhs[o * chans_in:(o + 1) * chans_in, row:row + chans] = w_ref[9 * ix + o, :, pl.ds(at, chans)]
                if offset_x == 0:
                    rhs[row:row + chans, :] = blocks[k][...]
                elif offset_x == 1:
                    rhs[row:row + chans, :size] = halos[k][:, :size]
                    rhs[row:row + chans, size:] = blocks[k][:, :(slab - 1) * size]
                else:
                    rhs[row:row + chans, :(slab - 1) * size] = blocks[k][:, size:]
                    rhs[row:row + chans, (slab - 1) * size:] = halos[k][:, size:]

    at = pl.multiple_of(plane * size, size)
    total = None if first else before[...]
    for iz, offset_z in enumerate(OFFSETS):
        over_y = None
        for iy, offset_y in enumerate(OFFSETS):
            row = (3 * iy + iz) * chans_in
            part = jnp.dot(lhs[row:row + chans_in, :], rhs[:, pl.ds(at, size)], preferred_element_type=jnp.float32)
            part = shift_y(part, offset_y)
            over_y = part if over_y is None else over_y + part
        over_y = shift_z(over_y, offset_z)
        total = over_y if total is None else total + over_y
    value = total.astype(out_ref.dtype)
    if first:
        out_ref[...] = value
    else:
        for p in range(slab):

            @pl.when(plane == p)
            def _():
                out_ref[:, p, :] = value


def backward(position, sources, blocks, halos, w, before, slab, out_dtype):
    number = len(blocks)
    chans, cells = blocks[0].shape
    chans_in = w.shape[1]
    size = cells // slab
    first = before is None
    whole = lambda a: pl.BlockSpec(a.shape, lambda n, s: (0,) * a.ndim, pipeline_mode=pl.Buffered(1))
    each = pl.BlockSpec((chans_in, size), lambda n, s: (0, n))
    out = jax.ShapeDtypeStruct((chans_in, cells) if first else (chans_in, slab, size), out_dtype)
    args = (*halos, *blocks, w) + (() if first else (before,))
    return pl.pallas_call(
        functools.partial(backward_kernel, slab, sources, first),
        grid_spec=pltpu.PrefetchScalarGridSpec(
            num_scalar_prefetch=1, grid=(slab,),
            in_specs=[whole(a) for a in args[:2 * number + 1]] + ([] if first else [each]),
            out_specs=each if first else whole(out),
            scratch_shapes=[pltpu.VMEM((9 * chans_in, 3 * number * chans), jnp.bfloat16),
                            pltpu.VMEM((3 * number * chans, cells), jnp.bfloat16)]),
        out_shape=out,
        compiler_params=pltpu.CompilerParams(vmem_limit_bytes=BACKWARD_VMEM),
        cost_estimate=pl.CostEstimate(flops=2*27*chans*chans_in*cells*number, bytes_accessed=w.size*2+chans_in*cells*4, transcendentals=0),
        name="backward",
    )(position, *args)


def padded(block, sides, width):
    for axis, dim in sides:
        count = lax.axis_size(axis)
        forward_ring = [(i, (i + 1) % count) for i in range(count)]
        backward_ring = [(target, source) for source, target in forward_ring]
        low = lax.ppermute(
            lax.slice_in_dim(block, block.shape[dim] - width, None, axis=dim), axis, forward_ring
        )
        high = lax.ppermute(lax.slice_in_dim(block, 0, width, axis=dim), axis, backward_ring)
        block = jnp.concatenate([low, block, high], axis=dim)
    return block


def stack_yz(block, rows_y):
    chans, slab_len, plane_size = block.shape
    shaped = block.reshape(chans, slab_len, rows_y, NZ)
    pieces = []
    for offset_y in OFFSETS:
        for offset_z in OFFSETS:
            pieces.append(jnp.roll(shaped, (-offset_y, -offset_z), axis=(2, 3)))
    return jnp.stack(pieces).reshape(9 * chans, slab_len * plane_size)


def general(inputs, weights, out_grad):
    chans_in, slab_len, plane_size = inputs.shape
    chans_out = out_grad.shape[0]
    full_out = weights.shape[2]
    rows_y = plane_size // NZ
    cell_count = slab_len * plane_size
    halo_in = padded(inputs, (("slab", 1),), 1)
    grad_all = lax.all_gather(out_grad, "chan", axis=0, tiled=True)
    halo_grad = padded(grad_all, (("slab", 1),), 1)
    running = jnp.zeros((full_out, cell_count), jnp.float32)
    for index_x, offset_x in enumerate(OFFSETS):
        columns = stack_yz(halo_in[:, 1 + offset_x : 1 + offset_x + slab_len], rows_y)
        weight_x = weights[9 * index_x : 9 * index_x + 9].reshape(9 * chans_in, full_out)
        running = running + lax.dot_general(
            weight_x, columns, (((0,), (0,)), ((), ())), preferred_element_type=jnp.float32
        )
    own_rows = lax.psum_scatter(running, "chan", scatter_dimension=0, tiled=True)
    conv_out = own_rows.astype(jnp.bfloat16).reshape(chans_out, slab_len, plane_size)
    running_grad = jnp.zeros((chans_in, slab_len, rows_y, NZ), jnp.float32)
    for index_x, offset_x in enumerate(OFFSETS):
        plane_x = halo_grad[:, 1 - offset_x : 1 - offset_x + slab_len].reshape(full_out, cell_count)
        weight_x = weights[9 * index_x : 9 * index_x + 9].reshape(9 * chans_in, full_out)
        product = lax.dot_general(
            weight_x, plane_x, (((1,), (0,)), ((), ())), preferred_element_type=jnp.float32
        )
        product = product.reshape(9, chans_in, slab_len, rows_y, NZ)
        for index_y, offset_y in enumerate(OFFSETS):
            for index_z, offset_z in enumerate(OFFSETS):
                running_grad = running_grad + jnp.roll(
                    product[3 * index_y + index_z], (offset_y, offset_z), axis=(2, 3)
                )
    input_grad = running_grad.reshape(chans_in, slab_len, plane_size).astype(jnp.bfloat16)
    return (conv_out, input_grad)


def edge_planes(block, size):
    count = lax.axis_size("slab")
    first, last = block[:, :size], block[:, block.shape[1] - size :]
    upward = [(i, (i + 1) % count) for i in range(count)]
    if count <= 2:
        return lax.ppermute(jnp.concatenate([last, first], axis=1), "slab", upward)
    downward = [(target, source) for source, target in upward]
    low, high = lax.ppermute(last, "slab", upward), lax.ppermute(first, "slab", downward)
    return jnp.concatenate([low, high], axis=1)


LINE = 4
TOP = 32768.0
ROWS, LANES = 8, 128


def tiles(block):
    rows, columns = block.shape
    split = block.reshape(rows // ROWS, ROWS, columns // LANES, LANES)
    return split.transpose(0, 2, 1, 3).reshape(-1, LANES)


def untiled(block, rows):
    split = block.reshape(rows // ROWS, -1, ROWS, LANES)
    return split.transpose(0, 2, 1, 3).reshape(rows, -1)


def scale_of(marks):
    marks = marks.astype(jnp.float32)
    return sum(marks[2 * i : 2 * i + 1] * marks[2 * i + 1 : 2 * i + 2] for i in range(LINE))


def pack(total, marks):
    scaled = (total * (TOP / scale_of(marks))).astype(jnp.float16)
    return jnp.concatenate([scaled, marks], axis=0)


def unpack(parcel):
    return parcel[:-ROWS].astype(jnp.float32) * (scale_of(parcel[-ROWS:]) * (1.0 / TOP))


def line_of_four(inputs, weights, out_grad):
    shape = inputs.shape
    chans, slab_len, size = shape
    slabs = lax.axis_size("slab")
    place = lax.axis_index("chan")
    position = place.reshape(1)
    inner = (place == 1) | (place == 2)

    def swap_ends(block):
        return lax.ppermute(block, "chan", [(0, 1), (1, 0), (2, 3), (3, 2)])

    def swap_middle(block):
        pairs = []
        for slab in range(slabs):
            other = (slab + 1) % slabs
            pairs += [(slabs + slab, 2 * slabs + slab), (2 * slabs + slab, slabs + slab)]
            pairs += [(end * slabs + slab, end * slabs + other) for end in (0, 3)]
        return lax.ppermute(block, ("chan", "slab"), pairs)

    def partial_or_cotangent(partial, marks, cotangent):
        cotangent = tiles(cotangent).astype(jnp.float32)
        bound = jnp.maximum(jnp.max(jnp.abs(cotangent), axis=0, keepdims=True) * 1.01, 2.0**-14)
        row = lax.broadcasted_iota(jnp.int32, marks.shape, 0)
        bounds = jnp.where(row == 0, bound, jnp.where(row == 1, 1.0, 0.0)).astype(jnp.float16)
        return pack(jnp.where(inner, cotangent, partial), jnp.where(inner, bounds, marks))

    def sum_with(partial, marks, parcel, counts=True):
        others = jnp.where(counts, parcel[-ROWS:], jnp.zeros_like(marks))
        theirs = parcel[:-ROWS].astype(jnp.float32) * (scale_of(others) * (1.0 / TOP))
        return pack(partial + theirs, marks + others)

    def cotangent_of(parcel):
        return untiled(unpack(parcel).astype(jnp.bfloat16), chans)

    grad = out_grad.reshape(chans, slab_len * size)
    field = inputs.reshape(chans, slab_len * size)
    ends_1 = swap_ends(grad)
    middle_1 = swap_middle(grad)
    field_edges = edge_planes(field, size)
    grad_edges = edge_planes(grad, size)
    (first,), first_marks = forward(position, (first_sum,), field, field_edges, weights, slab_len)
    first = tiles(first)
    first_marks = first_marks.astype(jnp.float16)

    middle_2 = swap_middle(ends_1)
    parcel = partial_or_cotangent(first, first_marks, middle_1)
    parcel, position_2 = lax.optimization_barrier((parcel, position))
    ends_2 = swap_ends(parcel)
    second_edges = edge_planes(ends_1, size)
    partials, marks = forward(
        position_2, (second_sum, third_sum, own_place), field, field_edges, weights, slab_len
    )
    second, third, own = (tiles(partial) for partial in partials)
    marks = marks.astype(jnp.float16)

    ends_3 = swap_ends(partial_or_cotangent(second, marks, middle_2))
    middle_3 = swap_middle(sum_with(first, first_marks, ends_2))
    grad_half = backward(
        position, (own_place, second_place), (grad, ends_1), (grad_edges, second_edges),
        weights, None, slab_len, jnp.float32,
    )
    grad_2 = jnp.where(inner, middle_1, cotangent_of(ends_2))
    edges_2 = edge_planes(grad_2, size)

    parcel = sum_with(third, marks, middle_3, inner)
    ends_4 = swap_ends(parcel)
    middle_4 = swap_middle(sum_with(second, marks, ends_3))
    _, ends_3, middle_2 = lax.optimization_barrier((parcel, ends_3, middle_2))
    grad_3 = jnp.where(inner, middle_2, cotangent_of(ends_3))
    edges_3 = edge_planes(grad_3, size)
    input_grad = backward(
        position, (third_place, fourth_place), (grad_2, grad_3), (edges_2, edges_3),
        weights, grad_half, slab_len, jnp.bfloat16,
    )
    conv_out = own + unpack(ends_4) + jnp.where(inner, unpack(middle_4), 0.0)
    conv_out = untiled(conv_out.astype(jnp.bfloat16), chans)
    return conv_out.reshape(shape), input_grad


def first_sum(place):
    return jnp.where(place < 2, 3, 0)


def second_sum(place):
    return jnp.where(place < 2, 2, 1)


def third_sum(place):
    return place ^ 1


def own_place(place):
    return place


def second_place(place):
    return place ^ 1


def third_place(place):
    return jnp.where(place < 2, 2, 1)


def fourth_place(place):
    return jnp.where(place < 2, 3, 0)


def chosen(inputs, weights, out_grad):
    chans, size = inputs.shape[0], inputs.shape[2]
    line = lax.axis_size("chan") == 4 and weights.shape[2] == 4 * chans and out_grad.shape[0] == chans
    if line and chans % 128 == 0 and size % 128 == 0:
        return line_of_four(inputs, weights, out_grad)
    return general(inputs, weights, out_grad)


def solution(mesh):
    in_specs = (
        P(("batch", "chan"), "slab", None),
        P(None, "chan", None),
        P(("batch", "chan"), "slab", None),
    )
    out_specs = (P(("batch", "chan"), "slab", None), P(("batch", "chan"), "slab", None))
    return jax.shard_map(chosen, mesh=mesh, in_specs=in_specs, out_specs=out_specs, check_vma=False)
```
